32 devices in a mesh: rep: 2 (over x), exp: 2 (over core), tp: 8 (over z, y).
Axes of the slice: x: 2, y: 2, z: 4, core: 2. Of those that a mesh axis runs over, the one named last changes fastest.
Arguments:
- tokens: bfloat16 [128, 4096], P(('rep', 'exp', 'tp')), parts along dimension 0, may hold values from -6 to 6
- expert_ids: int32 [128, 2], P(('rep', 'exp', 'tp')), parts along dimension 0, may hold values from 0 to 3, all different within a row; in each aligned block of 4 rows (0 to 3, 4 to 7, ...) at most 4 rows name the same one
- gate_ints: int32 [128, 2], P(('rep', 'exp', 'tp')), parts along dimension 0, may hold values from 16 to 240, as said below
- gate_weight: bfloat16 [4, 4096, 14336], P('exp', None, 'tp'), may hold values from -0.09375 to 0.09375
- up_weight: bfloat16 [4, 4096, 14336], P('exp', None, 'tp'), may hold values from -0.09375 to 0.09375
- down_weight: bfloat16 [4, 14336, 4096], P('exp', 'tp'), may hold values from -0.046875 to 0.046875
Outputs:
- mixed: bfloat16 [128, 4096], P(('rep', 'exp', 'tp')), parts along dimension 0
The draws below stay inside these ranges and needn't reach their ends.
There are 2 independent parts, one for each index of `rep`. The reference program is written for one: setup_inputs(seed, part) draws one part's arguments, and reference() takes and returns one part's arrays. A program takes and returns all parts, laid end to end along the dimension named above; an argument that names none is the same for every part. Nothing has to cross between parts.
Inputs may be any that keep to these rules, and one draw needn't show every extreme that they name: `expert_ids`: each row names two different experts. Among the 4 rows of one device an expert is named at most 4 times, and exactly that often on some device. `gate_ints`: the two entries of a row sum to 256.
All inputs are finite; a program needn't handle non-finite values.
Results may differ from the reference program's by a relative error of at most 0.0049.
Values may be sent and summed in bfloat16 or wider, within the bound.
A program may use at most 128 MiB of HBM per device.

```python
import math
import jax
import jax.numpy as jnp
import numpy as np
from jax import lax

D = 4096
FF = 14336
TOK_DEV = 4
EXPERTS = 4
TOKENS = 64


def draw_gate_ints(key, part):
    first = jax.random.randint(key, (TOKENS,), 16, 241)
    first = first.at[0].set(16)
    return jnp.stack([first, 256 - first], axis=1).astype(jnp.int32)


def block_scale(stream_key, shape, pieces, smallest, largest):
    gain = 1.0
    for axis_at, blocks in pieces:
        steps = jax.random.uniform(jax.random.fold_in(jax.random.fold_in(stream_key, 6), axis_at), (blocks,), jnp.float32, smallest / len(pieces), largest / len(pieces))
        gain = gain * jnp.repeat(jnp.exp(steps), shape[axis_at] // blocks).reshape((-1,) + (1,) * (len(shape) - 1 - axis_at))
    return gain


def assign_block(key, own, number, rows, amount, top, bound, slope):
    sequence = jax.random.permutation(key, amount)
    crowded, usual = load_shares(amount, rows * top, bound, slope, True), load_shares(amount, rows * top, bound, slope, False)
    places = jnp.arange(amount)

    def named(tallies, turn):
        used = int((tallies > 0).sum())
        fixed = max(1, used // 4)
        passed = fixed + (places - fixed + turn * (used - fixed)) % max(1, amount - fixed)
        return jnp.zeros((amount,), jnp.int32).at[sequence[jnp.where(places < fixed, places, passed)]].set(jnp.asarray(tallies, jnp.int32))

    tallies = jnp.where(number % 4 == 0, named(crowded, number // 4), named(usual, number - number // 4 - 1))
    mixed = jax.random.permutation(jax.random.fold_in(own, 3), amount)
    giver, sink = mixed[0:amount // 2 * 2:2], mixed[1:amount // 2 * 2:2]
    slack = jnp.minimum(tallies[giver] - 1, bound - tallies[sink]) // 2
    slack = jnp.where((giver == sequence[0]) | (sink == sequence[0]) | (tallies[sink] == 0), 0, jnp.maximum(slack, 0))
    passed = jax.random.randint(jax.random.fold_in(own, 4), (amount // 2,), 0, 1 << 20) % (slack + 1)
    tallies = tallies.at[giver].add(-passed).at[sink].add(passed)
    items = jnp.searchsorted(jnp.cumsum(tallies), jnp.arange(rows * top), side="right").astype(jnp.int32)
    table = items.reshape(top, rows).T
    table = table[jax.random.permutation(jax.random.fold_in(own, 1), rows)]
    turn = jax.random.randint(jax.random.fold_in(own, 2), (rows, 1), 0, top)
    return jnp.take_along_axis(table, (jnp.arange(top)[None, :] + turn) % top, axis=1)


def load_shares(amount, total, bound, lean, full):
    loads = [(1 << 20) // math.isqrt(grade ** lean) + 1 for grade in range(1, amount + 1)]
    largest = bound if full else min(bound, max(-(-total // amount), total * loads[0] // sum(loads)))
    least = 1 if total - largest >= amount - 1 else 0
    given, spare = [largest] + [least] * (amount - 1), total - largest - least * (amount - 1)
    while spare > 0:
        candidates = [i for i in range(1, amount) if given[i] < largest] or [i for i in range(1, amount) if given[i] < bound]
        whole, left = sum([loads[i] for i in candidates]), spare
        for i in candidates:
            more = min(bound - given[i], max(1, left * loads[i] // whole), spare)
            given[i] = given[i] + more
            spare = spare - more
    return np.array(given)


def gaussian(key, extent, width, bound, pieces=(), kind=jnp.bfloat16):
    loudness = block_scale(key, extent, pieces, -0.22, 0.18) if pieces else 1.0
    drawn = jax.random.normal(key, extent, jnp.float32) * width * loudness
    return jnp.minimum(jnp.maximum(drawn, -bound), bound).astype(kind)


def setup_inputs(seed: int = 0, part: int = 0) -> dict:
    seeds = jax.random.split(jax.random.key(seed), 7)
    part_keys = jax.random.split(jax.random.fold_in(seeds[6], part), 7)
    tokens = gaussian(part_keys[0], (TOKENS, D), 1.0, 6.0, ((0, 16),))
    expert_ids_keys = jax.random.split(jax.random.fold_in(part_keys[1], 1), TOKENS // TOK_DEV)
    expert_ids_turns = jax.random.permutation(jax.random.fold_in(part_keys[1], 3), TOKENS // TOK_DEV)
    expert_ids = jax.vmap(lambda own, number: assign_block(jax.random.fold_in(part_keys[1], 2), own, number, TOK_DEV, EXPERTS, 2, TOK_DEV, 1))(expert_ids_keys, expert_ids_turns).reshape((TOKENS, 2))
    gate_ints = draw_gate_ints(jax.random.fold_in(jax.random.fold_in(seeds[6], part), 71), part)
    gate_weight = gaussian(seeds[3], (EXPERTS, D, FF), D ** -0.5, 0.09375, ((0, 2), (2, 8)))
    up_weight = gaussian(seeds[4], (EXPERTS, D, FF), D ** -0.5, 0.09375, ((0, 2), (2, 8)))
    down_weight = gaussian(seeds[5], (EXPERTS, FF, D), FF ** -0.5, 0.046875, ((0, 2), (1, 8)))
    return dict(tokens=tokens, expert_ids=expert_ids, gate_ints=gate_ints, gate_weight=gate_weight, up_weight=up_weight, down_weight=down_weight)


def reference(tokens, expert_ids, gate_ints, gate_weight, up_weight, down_weight):
    inputs = tokens.astype(jnp.float32)
    gates = gate_ints.astype(jnp.float32) / 256.0

    def accumulate(index, total):
        w_gate = gate_weight[index].astype(jnp.float32)
        w_up = up_weight[index].astype(jnp.float32)
        w_down = down_weight[index].astype(jnp.float32)
        gate = jnp.dot(inputs, w_gate, preferred_element_type=jnp.float32)
        upper = jnp.dot(inputs, w_up, preferred_element_type=jnp.float32)
        hidden = (jax.nn.silu(gate) * upper).astype(jnp.bfloat16)
        output = jnp.dot(hidden.astype(jnp.float32), w_down, preferred_element_type=jnp.float32)
        weight = jnp.sum(jnp.where(expert_ids == index, gates, 0.0), axis=1)
        return total + weight[:, None] * output

    start = jnp.zeros((TOKENS, D), jnp.float32)
    total = lax.fori_loop(0, EXPERTS, accumulate, start)
    return total.astype(jnp.bfloat16)
```

```python
import functools

import jax
import jax.numpy as jnp
from jax import lax
from jax.experimental import pallas as pl
from jax.experimental.pallas import tpu as pltpu
from jax.sharding import PartitionSpec as P

MESH = pl.DeviceIdType.MESH
LANES = 128
VMEM_BYTES = 67043328


def kernel(
    nt, kb, cw, gu_slots, dn_slots,
    ids_ref, gates_ref, tok_ref, gw_ref, uw_ref, dw_ref, out_ref,
    xg, stage, x, wst, acc_g, acc_u, h, gu_buf, dn_buf,
    part, ex_send, ex_recv, tp_send, tp_recv,
    gu_sem, dn_sem, ga_send, ga_fwd, ga_recv, ex_ssem, ex_rsem, tp_ssem, tp_rsem,
):
    e = lax.axis_index("exp")
    t = lax.axis_index("tp")
    other = 1 - e
    me = e * nt + t
    rows, width = tok_ref.shape
    experts, _, hidden = gw_ref.shape
    tokens = x.shape[1]
    half = tokens // 2
    nk = width // kb
    nc = width // cw
    gu_steps = experts * nk

    def gu_copies(i, slot):
        l = i // nk
        k0 = pl.multiple_of((i % nk) * kb, kb)
        return [
            pltpu.make_async_copy(
                ref.at[l, pl.ds(k0, kb), :], gu_buf.at[slot, m], gu_sem.at[slot, m]
            )
            for m, ref in enumerate((gw_ref, uw_ref))
        ]

    def dn_copies(c, slot):
        c0 = pl.multiple_of(c * cw, cw)
        return [
            pltpu.make_async_copy(
                dw_ref.at[l, :, pl.ds(c0, cw)], dn_buf.at[slot, l], dn_sem.at[slot, l]
            )
            for l in range(experts)
        ]

    def first(i, carry):
        for copy in gu_copies(i, i):
            copy.start()
        return carry

    lax.fori_loop(0, gu_slots, first, 0)

    barrier = pltpu.get_barrier_semaphore()

    def greet(d, carry):
        pl.semaphore_signal(
            barrier, inc=1, device_id={"tp": (t + d) % nt}, device_id_type=MESH
        )
        return carry

    lax.fori_loop(1, nt, greet, 0)
    pl.semaphore_signal(barrier, inc=1, device_id={"exp": other}, device_id_type=MESH)

    lane = lax.broadcasted_iota(jnp.int32, (rows, LANES), 1)
    sub = lax.broadcasted_iota(jnp.int32, (rows, LANES), 0)
    weight = jnp.zeros((rows, LANES), jnp.float32)
    for r in range(rows):
        for k in range(ids_ref.shape[0]):
            value = gates_ref[k, r].astype(jnp.float32) * (1.0 / 256.0)
            weight += jnp.where((sub == r) & (lane == ids_ref[k, r]), value, 0.0)
    xg[me, :, :width] = tok_ref[...]
    xg[me, :, width:] = weight.astype(jnp.bfloat16)

    pl.semaphore_wait(barrier, nt)

    def to_other(tt):
        slot = e * nt + tt
        return pltpu.make_async_remote_copy(
            src_ref=xg.at[slot], dst_ref=xg.at[slot],
            send_sem=ga_fwd.at[tt], recv_sem=ga_recv.at[slot],
            device_id={"exp": other}, device_id_type=MESH,
        )

    def to_tp(d):
        return pltpu.make_async_remote_copy(
            src_ref=xg.at[me], dst_ref=xg.at[me],
            send_sem=ga_send.at[d], recv_sem=ga_recv.at[me],
            device_id={"tp": (t + d) % nt}, device_id_type=MESH,
        )

    def from_slot(slot):
        return pltpu.make_async_remote_copy(
            src_ref=xg.at[slot], dst_ref=xg.at[slot],
            send_sem=ga_send.at[0], recv_sem=ga_recv.at[slot],
            device_id={"exp": other}, device_id_type=MESH,
        )

    def push(d, carry):
        to_tp(d).start()
        return carry

    lax.fori_loop(1, nt, push, 0)
    to_other(t).start()

    def relay(d, carry):
        source = (t + nt - d) % nt
        from_slot(e * nt + source).wait_recv()
        to_other(source).start()
        return carry

    lax.fori_loop(1, nt, relay, 0)

    def arrive(tt, carry):
        from_slot(other * nt + tt).wait_recv()
        return carry

    lax.fori_loop(0, nt, arrive, 0)

    group = stage.shape[0] // rows

    def lay(g, carry):
        for i in range(group):
            stage[i * rows:(i + 1) * rows, :] = xg[g * group + i].astype(jnp.float32)
        r0 = pl.multiple_of(g * group * rows, group * rows)
        for k in range(nk):
            x[k, pl.ds(r0, group * rows), :] = stage[:, k * kb:(k + 1) * kb].astype(jnp.bfloat16)
        wst[pl.ds(r0, group * rows), :] = stage[:, width:]
        return carry

    lax.fori_loop(0, tokens // (group * rows), lay, 0)

    tiles = [(n, min(256, hidden - n)) for n in range(0, hidden, 256)]

    def gu_step(i, carry):
        slot = i % gu_slots
        k = i % nk
        for copy in gu_copies(i, slot):
            copy.wait()

        @pl.when(k == 0)
        def _():
            acc_g[...] = jnp.zeros_like(acc_g)
            acc_u[...] = jnp.zeros_like(acc_u)

        xk = x[k]
        for n, size in tiles:
            for m, acc in enumerate((acc_g, acc_u)):
                acc[:, n:n + size] += jnp.dot(
                    xk, gu_buf[slot, m, :, n:n + size], preferred_element_type=jnp.float32
                )

        @pl.when(k == nk - 1)
        def _():
            for n, size in tiles:
                gate = acc_g[:, n:n + size]
                silu = gate / (1.0 + jnp.exp(-gate))
                h[i // nk, :, n:n + size] = (silu * acc_u[:, n:n + size]).astype(jnp.bfloat16)

        later = i + gu_slots

        @pl.when(later < gu_steps)
        def _():
            for copy in gu_copies(later, slot):
                copy.start()

        column = later - gu_steps

        @pl.when((column >= 0) & (column < dn_slots))
        def _():
            for copy in dn_copies(column, column):
                copy.start()

        return carry

    lax.fori_loop(0, gu_steps, gu_step, 0)

    lanes = lax.broadcasted_iota(jnp.int32, (tokens, LANES), 1)
    scales = [
        jnp.sum(jnp.where(lanes == e * experts + l, wst[...], 0.0), axis=1, keepdims=True)
        for l in range(experts)
    ]

    def ex_copy(c):
        return pltpu.make_async_remote_copy(
            src_ref=ex_send.at[c], dst_ref=ex_recv.at[c],
            send_sem=ex_ssem.at[c], recv_sem=ex_rsem.at[c],
            device_id={"exp": other}, device_id_type=MESH,
        )

    def tp_copy(c, d):
        target = (t + d) % nt
        return pltpu.make_async_remote_copy(
            src_ref=tp_send.at[c, target], dst_ref=tp_recv.at[c, t],
            send_sem=tp_ssem.at[c, d], recv_sem=tp_rsem.at[c, t],
            device_id={"tp": target}, device_id_type=MESH,
        )

    def tp_from(c, source):
        return pltpu.make_async_remote_copy(
            src_ref=tp_send.at[c, source], dst_ref=tp_recv.at[c, source],
            send_sem=tp_ssem.at[c, 0], recv_sem=tp_rsem.at[c, source],
            device_id={"tp": source}, device_id_type=MESH,
        )

    def pass_on(c):
        ex_copy(c).wait_recv()
        total = part[c, e] + ex_recv[c].astype(jnp.float32)
        for j in range(nt):
            tp_send[c, j] = total[j * rows:(j + 1) * rows, :].astype(jnp.bfloat16)
        tp_recv[c, t] = tp_send[c, t]

        def send(d, carry):
            tp_copy(c, d).start()
            return carry

        lax.fori_loop(1, nt, send, 0)

    def dn_step(c, carry):
        slot = c % dn_slots
        for copy in dn_copies(c, slot):
            copy.wait()
        for n in range(0, cw, 256):
            size = min(256, cw - n)
            total = jnp.zeros((tokens, size), jnp.float32)
            for l in range(experts):
                total += scales[l] * jnp.dot(
                    h[l], dn_buf[slot, l, :, n:n + size], preferred_element_type=jnp.float32
                )
            part[c, 0, :, n:n + size] = total[:half]
            part[c, 1, :, n:n + size] = total[half:]
        ex_send[c] = part[c, other].astype(jnp.bfloat16)
        ex_copy(c).start()
        later = c + dn_slots

        @pl.when(later < nc)
        def _():
            for copy in dn_copies(later, slot):
                copy.start()

        @pl.when(c > 0)
        def _():
            pass_on(c - 1)

        return carry

    lax.fori_loop(0, nc, dn_step, 0)
    pass_on(nc - 1)

    for c in range(nc):
        def collect(d, carry, c=c):
            tp_from(c, (t + nt - d) % nt).wait_recv()
            return carry

        lax.fori_loop(1, nt, collect, 0)
        total = tp_recv[c, 0].astype(jnp.float32)
        for j in range(1, nt):
            total += tp_recv[c, j].astype(jnp.float32)
        out_ref[:, c * cw:(c + 1) * cw] = total.astype(out_ref.dtype)

    def finish(d, carry):
        to_tp(d).wait_send()
        to_other((t + d) % nt).wait_send()

        def drain(c, inner):
            tp_copy(c, d).wait_send()
            return inner

        lax.fori_loop(0, nc, drain, 0)
        return carry

    lax.fori_loop(1, nt, finish, 0)
    to_other(t).wait_send()

    def drain_ex(c, carry):
        ex_copy(c).wait_send()
        return carry

    lax.fori_loop(0, nc, drain_ex, 0)


def body(tokens, expert_ids, gate_ints, gate_weight, up_weight, down_weight):
    rows, width = tokens.shape
    experts, _, hidden = gate_weight.shape
    nt = lax.axis_size("tp")
    slots = nt * lax.axis_size("exp")
    total = slots * rows
    kb = min(512, width)
    cw = min(512, width)
    nk, nc = width // kb, width // cw
    gu_slots = min(12, experts * nk)
    dn_slots = min(4, nc)
    bf16, f32 = jnp.bfloat16, jnp.float32
    vmem = pl.BlockSpec(memory_space=pltpu.VMEM)
    smem = pl.BlockSpec(memory_space=pltpu.SMEM)
    hbm = pl.BlockSpec(memory_space=pl.ANY)
    dma = pltpu.SemaphoreType.DMA
    return pl.pallas_call(
        functools.partial(kernel, nt, kb, cw, gu_slots, dn_slots),
        out_shape=jax.ShapeDtypeStruct((rows, width), bf16),
        in_specs=[smem, smem, vmem, hbm, hbm, hbm],
        out_specs=vmem,
        scratch_shapes=[
            pltpu.VMEM((slots, rows, width + LANES), bf16),
            pltpu.VMEM((16, width + LANES), f32),
            pltpu.VMEM((nk, total, kb), bf16),
            pltpu.VMEM((total, LANES), f32),
            pltpu.VMEM((total, hidden), f32),
            pltpu.VMEM((total, hidden), f32),
            pltpu.VMEM((experts, total, hidden), bf16),
            pltpu.VMEM((gu_slots, 2, kb, hidden), bf16),
            pltpu.VMEM((dn_slots, experts, hidden, cw), bf16),
            pltpu.VMEM((nc, 2, total // 2, cw), f32),
            pltpu.VMEM((nc, total // 2, cw), bf16),
            pltpu.VMEM((nc, total // 2, cw), bf16),
            pltpu.VMEM((nc, nt, rows, cw), bf16),
            pltpu.VMEM((nc, nt, rows, cw), bf16),
            dma((gu_slots, 2)),
            dma((dn_slots, experts)),
            dma((nt,)),
            dma((nt,)),
            dma((slots,)),
            dma((nc,)),
            dma((nc,)),
            dma((nc, nt)),
            dma((nc, nt)),
        ],
        compiler_params=pltpu.CompilerParams(
            collective_id=0, has_side_effects=True, vmem_limit_bytes=VMEM_BYTES
        ),
    )(expert_ids.T, gate_ints.T, tokens, gate_weight, up_weight, down_weight)


def solution(mesh):
    return jax.shard_map(
        body,
        mesh=mesh,
        in_specs=(
            P(("rep", "exp", "tp"), None),
            P(("rep", "exp", "tp"), None),
            P(("rep", "exp", "tp"), None),
            P("exp", None, "tp"),
            P("exp", None, "tp"),
            P("exp", "tp", None),
        ),
        out_specs=P(("rep", "exp", "tp"), None),
        check_vma=False,
    )
```

```python
import functools

import jax
import jax.numpy as jnp
from jax import lax
from jax.experimental import pallas as pl
from jax.experimental.pallas import tpu as pltpu
from jax.sharding import PartitionSpec as P

MESH = pl.DeviceIdType.MESH
LANES = 128
VMEM_BYTES = 67043328


def kernel(
    nt, fb, cw, gu_slots, dn_slots,
    ids_ref, gates_ref, tok_ref, gw_ref, uw_ref, dw_ref, out_ref,
    xg, stage, x, wst, h, gu_buf, dn_buf,
    part, ex_send, ex_recv, tp_send, tp_recv,
    gu_sem, dn_sem, ga_send, ga_fwd, ga_recv, ex_ssem, ex_rsem, tp_ssem, tp_rsem,
):
    e = lax.axis_index("exp")
    t = lax.axis_index("tp")
    other = 1 - e
    me = e * nt + t
    rows, width = tok_ref.shape
    experts, _, hidden = gw_ref.shape
    tokens = x.shape[0]
    half = tokens // 2
    nf = hidden // fb
    nc = width // cw
    gu_steps = experts * nf

    def gu_copies(i, slot):
        l = i // nf
        columns = pl.ds(pl.multiple_of((i % nf) * fb, fb), fb) if nf > 1 else slice(None)
        return [
            pltpu.make_async_copy(
                ref.at[l, :, columns], gu_buf.at[slot, m], gu_sem.at[slot, m]
            )
            for m, ref in enumerate((gw_ref, uw_ref))
        ]

    def dn_copies(c, slot):
        c0 = pl.multiple_of(c * cw, cw)
        return [
            pltpu.make_async_copy(
                dw_ref.at[l, :, pl.ds(c0, cw)], dn_buf.at[slot, l], dn_sem.at[slot, l]
            )
            for l in range(experts)
        ]

    def first(i, carry):
        for copy in gu_copies(i, i):
            copy.start()
        return carry

    lax.fori_loop(0, gu_slots, first, 0)

    barrier = pltpu.get_barrier_semaphore()

    def greet(d, carry):
        pl.semaphore_signal(
            barrier, inc=1, device_id={"tp": (t + d) % nt}, device_id_type=MESH
        )
        return carry

    lax.fori_loop(1, nt, greet, 0)
    pl.semaphore_signal(barrier, inc=1, device_id={"exp": other}, device_id_type=MESH)

    lane = lax.broadcasted_iota(jnp.int32, (rows, LANES), 1)
    sub = lax.broadcasted_iota(jnp.int32, (rows, LANES), 0)
    weight = jnp.zeros((rows, LANES), jnp.float32)
    for r in range(rows):
        for k in range(ids_ref.shape[0]):
            value = gates_ref[k, r].astype(jnp.float32) * (1.0 / 256.0)
            weight += jnp.where((sub == r) & (lane == ids_ref[k, r]), value, 0.0)
    xg[me, :, :width] = tok_ref[...]
    xg[me, :, width:] = weight.astype(jnp.bfloat16)

    pl.semaphore_wait(barrier, nt)

    def to_other(tt):
        slot = e * nt + tt
        return pltpu.make_async_remote_copy(
            src_ref=xg.at[slot], dst_ref=xg.at[slot],
            send_sem=ga_fwd.at[tt], recv_sem=ga_recv.at[slot],
            device_id={"exp": other}, device_id_type=MESH,
        )

    def to_tp(d):
        return pltpu.make_async_remote_copy(
            src_ref=xg.at[me], dst_ref=xg.at[me],
            send_sem=ga_send.at[d], recv_sem=ga_recv.at[me],
            device_id={"tp": (t + d) % nt}, device_id_type=MESH,
        )

    def from_slot(slot):
        return pltpu.make_async_remote_copy(
            src_ref=xg.at[slot], dst_ref=xg.at[slot],
            send_sem=ga_send.at[0], recv_sem=ga_recv.at[slot],
            device_id={"exp": other}, device_id_type=MESH,
        )

    def push(d, carry):
        to_tp(d).start()
        return carry

    lax.fori_loop(1, nt, push, 0)
    to_other(t).start()

    def relay(d, carry):
        source = (t + nt - d) % nt
        from_slot(e * nt + source).wait_recv()
        to_other(source).start()
        return carry

    lax.fori_loop(1, nt, relay, 0)

    def arrive(tt, carry):
        from_slot(other * nt + tt).wait_recv()
        return carry

    lax.fori_loop(0, nt, arrive, 0)

    group = stage.shape[0] // rows

    def lay(g, carry):
        for i in range(group):
            stage[i * rows:(i + 1) * rows, :] = xg[g * group + i].astype(jnp.float32)
        r0 = pl.multiple_of(g * group * rows, group * rows)
        x[pl.ds(r0, group * rows), :] = stage[:, :width].astype(jnp.bfloat16)
        wst[pl.ds(r0, group * rows), :] = stage[:, width:]
        return carry

    lax.fori_loop(0, tokens // (group * rows), lay, 0)

    def gu_step(i, carry):
        slot = i % gu_slots
        for copy in gu_copies(i, slot):
            copy.wait()
        gate, upper = (
            jnp.dot(x[...], gu_buf[slot, m], preferred_element_type=jnp.float32) for m in range(2)
        )
        columns = pl.ds(pl.multiple_of((i % nf) * fb, fb), fb) if nf > 1 else slice(None)
        h[i // nf, :, columns] = (gate / (1.0 + jnp.exp(-gate)) * upper).astype(jnp.bfloat16)
        later = i + gu_slots

        @pl.when(later < gu_steps)
        def _():
            for copy in gu_copies(later, slot):
                copy.start()

        column = later - gu_steps

        @pl.when((column >= 0) & (column < dn_slots))
        def _():
            for copy in dn_copies(column, column):
                copy.start()

        return carry

    lax.fori_loop(0, gu_steps, gu_step, 0)

    lanes = lax.broadcasted_iota(jnp.int32, (tokens, LANES), 1)
    scales = [
        jnp.sum(jnp.where(lanes == e * experts + l, wst[...], 0.0), axis=1, keepdims=True)
        for l in range(experts)
    ]

    def ex_copy(c):
        return pltpu.make_async_remote_copy(
            src_ref=ex_send.at[c], dst_ref=ex_recv.at[c],
            send_sem=ex_ssem.at[c], recv_sem=ex_rsem.at[c],
            device_id={"exp": other}, device_id_type=MESH,
        )

    def tp_copy(c, d):
        target = (t + d) % nt
        return pltpu.make_async_remote_copy(
            src_ref=tp_send.at[c, target], dst_ref=tp_recv.at[c, t],
            send_sem=tp_ssem.at[c, d], recv_sem=tp_rsem.at[c, t],
            device_id={"tp": target}, device_id_type=MESH,
        )

    def tp_from(c, source):
        return pltpu.make_async_remote_copy(
            src_ref=tp_send.at[c, source], dst_ref=tp_recv.at[c, source],
            send_sem=tp_ssem.at[c, 0], recv_sem=tp_rsem.at[c, source],
            device_id={"tp": source}, device_id_type=MESH,
        )

    def pass_on(c):
        ex_copy(c).wait_recv()
        total = part[c, e] + ex_recv[c].astype(jnp.float32)
        for j in range(nt):
            tp_send[c, j] = total[j * rows:(j + 1) * rows, :].astype(jnp.bfloat16)
        tp_recv[c, t] = tp_send[c, t]

        def send(d, carry):
            tp_copy(c, d).start()
            return carry

        lax.fori_loop(1, nt, send, 0)

    def dn_step(c, carry):
        slot = c % dn_slots
        for copy in dn_copies(c, slot):
            copy.wait()
        for n in range(0, cw, 256):
            size = min(256, cw - n)
            total = jnp.zeros((tokens, size), jnp.float32)
            for l in range(experts):
                total += scales[l] * jnp.dot(
                    h[l], dn_buf[slot, l, :, n:n + size], preferred_element_type=jnp.float32
                )
            part[c, 0, :, n:n + size] = total[:half]
            part[c, 1, :, n:n + size] = total[half:]
        ex_send[c] = part[c, other].astype(jnp.bfloat16)
        ex_copy(c).start()
        later = c + dn_slots

        @pl.when(later < nc)
        def _():
            for copy in dn_copies(later, slot):
                copy.start()

        @pl.when(c > 0)
        def _():
            pass_on(c - 1)

        return carry

    lax.fori_loop(0, nc, dn_step, 0)
    pass_on(nc - 1)

    for c in range(nc):
        def collect(d, carry, c=c):
            tp_from(c, (t + nt - d) % nt).wait_recv()
            return carry

        lax.fori_loop(1, nt, collect, 0)
        total = tp_recv[c, 0].astype(jnp.float32)
        for j in range(1, nt):
            total += tp_recv[c, j].astype(jnp.float32)
        out_ref[:, c * cw:(c + 1) * cw] = total.astype(out_ref.dtype)

    def finish(d, carry):
        to_tp(d).wait_send()
        to_other((t + d) % nt).wait_send()

        def drain(c, inner):
            tp_copy(c, d).wait_send()
            return inner

        lax.fori_loop(0, nc, drain, 0)
        return carry

    lax.fori_loop(1, nt, finish, 0)
    to_other(t).wait_send()

    def drain_ex(c, carry):
        ex_copy(c).wait_send()
        return carry

    lax.fori_loop(0, nc, drain_ex, 0)


def body(tokens, expert_ids, gate_ints, gate_weight, up_weight, down_weight):
    rows, width = tokens.shape
    experts, _, hidden = gate_weight.shape
    nt = lax.axis_size("tp")
    slots = nt * lax.axis_size("exp")
    total = slots * rows
    fb = 256 if hidden % 256 == 0 else hidden
    cw = min(512, width)
    nf, nc = hidden // fb, width // cw
    gu_slots = min(10, experts * nf)
    dn_slots = min(4, nc)
    bf16, f32 = jnp.bfloat16, jnp.float32
    vmem = pl.BlockSpec(memory_space=pltpu.VMEM)
    smem = pl.BlockSpec(memory_space=pltpu.SMEM)
    hbm = pl.BlockSpec(memory_space=pl.ANY)
    dma = pltpu.SemaphoreType.DMA
    return pl.pallas_call(
        functools.partial(kernel, nt, fb, cw, gu_slots, dn_slots),
        out_shape=jax.ShapeDtypeStruct((rows, width), bf16),
        in_specs=[smem, smem, vmem, hbm, hbm, hbm],
        out_specs=vmem,
        scratch_shapes=[
            pltpu.VMEM((slots, rows, width + LANES), bf16),
            pltpu.VMEM((16, width + LANES), f32),
            pltpu.VMEM((total, width), bf16),
            pltpu.VMEM((total, LANES), f32),
            pltpu.VMEM((experts, total, hidden), bf16),
            pltpu.VMEM((gu_slots, 2, width, fb), bf16),
            pltpu.VMEM((dn_slots, experts, hidden, cw), bf16),
            pltpu.VMEM((nc, 2, total // 2, cw), f32),
            pltpu.VMEM((nc, total // 2, cw), bf16),
            pltpu.VMEM((nc, total // 2, cw), bf16),
            pltpu.VMEM((nc, nt, rows, cw), bf16),
            pltpu.VMEM((nc, nt, rows, cw), bf16),
            dma((gu_slots, 2)),
            dma((dn_slots, experts)),
            dma((nt,)),
            dma((nt,)),
            dma((slots,)),
            dma((nc,)),
            dma((nc,)),
            dma((nc, nt)),
            dma((nc, nt)),
        ],
        compiler_params=pltpu.CompilerParams(
            collective_id=0, has_side_effects=True, vmem_limit_bytes=VMEM_BYTES
        ),
    )(expert_ids.T, gate_ints.T, tokens, gate_weight, up_weight, down_weight)


def solution(mesh):
    return jax.shard_map(
        body,
        mesh=mesh,
        in_specs=(
            P(("rep", "exp", "tp"), None),
            P(("rep", "exp", "tp"), None),
            P(("rep", "exp", "tp"), None),
            P("exp", None, "tp"),
            P("exp", None, "tp"),
            P("exp", "tp", None),
        ),
        out_specs=P(("rep", "exp", "tp"), None),
        check_vma=False,
    )
```

```python
import functools

import jax
import jax.numpy as jnp
from jax import lax
from jax.experimental import pallas as pl
from jax.experimental.pallas import tpu as pltpu
from jax.sharding import PartitionSpec as P

MESH = pl.DeviceIdType.MESH
LANES = 128
VMEM_BYTES = 67043328


def kernel(
    nt, fb, cw, gu_slots, dn_slots,
    ids_ref, gates_ref, tok_ref, gw_ref, uw_ref, dw_ref, out_ref,
    xg, stage, x, wst, h, gu_buf, dn_buf,
    part, ex_send, ex_recv, tp_send, tp_recv,
    gu_sem, dn_sem, ga_send, ga_fwd, ga_recv, ex_ssem, ex_rsem, tp_ssem, tp_rsem,
):
    e = lax.axis_index("exp")
    t = lax.axis_index("tp")
    other = 1 - e
    me = e * nt + t
    rows, width = tok_ref.shape
    experts, _, hidden = gw_ref.shape
    tokens = x.shape[0]
    half = tokens // 2
    nf = hidden // fb
    nc = width // cw
    gu_steps = experts * nf

    def gu_copies(i, slot):
        l = i // nf
        columns = pl.ds(pl.multiple_of((i % nf) * fb, fb), fb) if nf > 1 else slice(None)
        return [
            pltpu.make_async_copy(
                ref.at[l, :, columns], gu_buf.at[slot, m], gu_sem.at[slot, m]
            )
            for m, ref in enumerate((gw_ref, uw_ref))
        ]

    def dn_copies(c, slot):
        c0 = pl.multiple_of(c * cw, cw)
        return [
            pltpu.make_async_copy(
                dw_ref.at[l, :, pl.ds(c0, cw)], dn_buf.at[slot, l], dn_sem.at[slot, l]
            )
            for l in range(experts)
        ]

    def first(i, carry):
        for copy in gu_copies(i, i):
            copy.start()
        return carry

    lax.fori_loop(0, gu_slots, first, 0)

    barrier = pltpu.get_barrier_semaphore()

    def greet(d, carry):
        pl.semaphore_signal(
            barrier, inc=1, device_id={"tp": (t + d) % nt}, device_id_type=MESH
        )
        return carry

    lax.fori_loop(1, nt, greet, 0)
    pl.semaphore_signal(barrier, inc=1, device_id={"exp": other}, device_id_type=MESH)

    lane = lax.broadcasted_iota(jnp.int32, (rows, LANES), 1)
    sub = lax.broadcasted_iota(jnp.int32, (rows, LANES), 0)
    weight = jnp.zeros((rows, LANES), jnp.float32)
    for r in range(rows):
        for k in range(ids_ref.shape[0]):
            value = gates_ref[k, r].astype(jnp.float32) * (1.0 / 256.0)
            weight += jnp.where((sub == r) & (lane == ids_ref[k, r]), value, 0.0)
    xg[me, :, :width] = tok_ref[...]
    xg[me, :, width:] = weight.astype(jnp.bfloat16)

    pl.semaphore_wait(barrier, nt)

    def to_other(tt):
        slot = e * nt + tt
        return pltpu.make_async_remote_copy(
            src_ref=xg.at[slot], dst_ref=xg.at[slot],
            send_sem=ga_fwd.at[tt], recv_sem=ga_recv.at[slot],
            device_id={"exp": other}, device_id_type=MESH,
        )

    def to_tp(d):
        return pltpu.make_async_remote_copy(
            src_ref=xg.at[me], dst_ref=xg.at[me],
            send_sem=ga_send.at[d], recv_sem=ga_recv.at[me],
            device_id={"tp": (t + d) % nt}, device_id_type=MESH,
        )

    def from_slot(slot):
        return pltpu.make_async_remote_copy(
            src_ref=xg.at[slot], dst_ref=xg.at[slot],
            send_sem=ga_send.at[0], recv_sem=ga_recv.at[slot],
            device_id={"exp": other}, device_id_type=MESH,
        )

    def push(d, carry):
        to_tp(d).start()
        return carry

    lax.fori_loop(1, nt, push, 0)
    to_other(t).start()

    def relay(d, carry):
        source = (t + nt - d) % nt
        from_slot(e * nt + source).wait_recv()
        to_other(source).start()
        return carry

    lax.fori_loop(1, nt, relay, 0)

    def arrive(tt, carry):
        from_slot(other * nt + tt).wait_recv()
        return carry

    lax.fori_loop(0, nt, arrive, 0)

    group = stage.shape[0] // rows

    def lay(g, carry):
        for i in range(group):
            stage[i * rows:(i + 1) * rows, :] = xg[g * group + i].astype(jnp.float32)
        r0 = pl.multiple_of(g * group * rows, group * rows)
        x[pl.ds(r0, group * rows), :] = stage[:, :width].astype(jnp.bfloat16)
        wst[pl.ds(r0, group * rows), :] = stage[:, width:]
        return carry

    lax.fori_loop(0, tokens // (group * rows), lay, 0)

    def gu_step(i, carry):
        slot = i % gu_slots
        for copy in gu_copies(i, slot):
            copy.wait()
        gate, upper = (
            jnp.dot(x[...], gu_buf[slot, m], preferred_element_type=jnp.float32) for m in range(2)
        )
        columns = pl.ds(pl.multiple_of((i % nf) * fb, fb), fb) if nf > 1 else slice(None)
        h[i // nf, :, columns] = (gate / (1.0 + jnp.exp(-gate)) * upper).astype(jnp.bfloat16)
        later = i + gu_slots

        @pl.when(later < gu_steps)
        def _():
            for copy in gu_copies(later, slot):
                copy.start()

        column = later - gu_steps

        @pl.when((column >= 0) & (column < dn_slots))
        def _():
            for copy in dn_copies(column, column):
                copy.start()

        return carry

    lax.fori_loop(0, gu_steps, gu_step, 0)

    lanes = lax.broadcasted_iota(jnp.int32, (tokens, LANES), 1)
    scales = [
        jnp.sum(jnp.where(lanes == e * experts + l, wst[...], 0.0), axis=1, keepdims=True)
        for l in range(experts)
    ]

    def ex_copy(c):
        return pltpu.make_async_remote_copy(
            src_ref=ex_send.at[c], dst_ref=ex_recv.at[c],
            send_sem=ex_ssem.at[c], recv_sem=ex_rsem.at[c],
            device_id={"exp": other}, device_id_type=MESH,
        )

    def tp_copy(c, d):
        target = (t + d) % nt
        return pltpu.make_async_remote_copy(
            src_ref=tp_send.at[c, target], dst_ref=tp_recv.at[c, t],
            send_sem=tp_ssem.at[c, d], recv_sem=tp_rsem.at[c, t],
            device_id={"tp": target}, device_id_type=MESH,
        )

    def tp_from(c, source):
        return pltpu.make_async_remote_copy(
            src_ref=tp_send.at[c, source], dst_ref=tp_recv.at[c, source],
            send_sem=tp_ssem.at[c, 0], recv_sem=tp_rsem.at[c, source],
            device_id={"tp": source}, device_id_type=MESH,
        )

    def pass_on(c):
        ex_copy(c).wait_recv()
        total = part[c, e] + ex_recv[c].astype(jnp.float32)
        for j in range(nt):
            tp_send[c, j] = total[j * rows:(j + 1) * rows, :].astype(jnp.bfloat16)
        tp_recv[c, t] = tp_send[c, t]

        def send(d, carry):
            tp_copy(c, d).start()
            return carry

        lax.fori_loop(1, nt, send, 0)

    def dn_step(c, carry):
        slot = c % dn_slots
        for copy in dn_copies(c, slot):
            copy.wait()
        for n in range(0, cw, 256):
            size = min(256, cw - n)
            total = jnp.zeros((tokens, size), jnp.float32)
            for l in range(experts):
                total += scales[l] * jnp.dot(
                    h[l], dn_buf[slot, l, :, n:n + size], preferred_element_type=jnp.float32
                )
            part[c, 0, :, n:n + size] = total[:half]
            part[c, 1, :, n:n + size] = total[half:]
        ex_send[c] = part[c, other].astype(jnp.bfloat16)
        ex_copy(c).start()
        later = c + dn_slots

        @pl.when(later < nc)
        def _():
            for copy in dn_copies(later, slot):
                copy.start()

        @pl.when(c > 0)
        def _():
            pass_on(c - 1)

        return carry

    lax.fori_loop(0, nc, dn_step, 0)
    pass_on(nc - 1)

    for c in range(nc):
        def collect(d, carry, c=c):
            tp_from(c, (t + nt - d) % nt).wait_recv()
            return carry

        lax.fori_loop(1, nt, collect, 0)
        total = tp_recv[c, 0].astype(jnp.float32)
        for j in range(1, nt):
            total += tp_recv[c, j].astype(jnp.float32)
        out_ref[:, c * cw:(c + 1) * cw] = total.astype(out_ref.dtype)

    def finish(d, carry):
        to_tp(d).wait_send()
        to_other((t + d) % nt).wait_send()

        def drain(c, inner):
            tp_copy(c, d).wait_send()
            return inner

        lax.fori_loop(0, nc, drain, 0)
        return carry

    lax.fori_loop(1, nt, finish, 0)
    to_other(t).wait_send()

    def drain_ex(c, carry):
        ex_copy(c).wait_send()
        return carry

    lax.fori_loop(0, nc, drain_ex, 0)


def body(tokens, expert_ids, gate_ints, gate_weight, up_weight, down_weight):
    rows, width = tokens.shape
    experts, _, hidden = gate_weight.shape
    nt = lax.axis_size("tp")
    slots = nt * lax.axis_size("exp")
    total = slots * rows
    fb = 256 if hidden % 256 == 0 else hidden
    cw = min(512, width)
    nf, nc = hidden // fb, width // cw
    gu_slots = min(8, experts * nf)
    dn_slots = min(7, nc)
    bf16, f32 = jnp.bfloat16, jnp.float32
    vmem = pl.BlockSpec(memory_space=pltpu.VMEM)
    smem = pl.BlockSpec(memory_space=pltpu.SMEM)
    hbm = pl.BlockSpec(memory_space=pl.ANY)
    dma = pltpu.SemaphoreType.DMA
    return pl.pallas_call(
        functools.partial(kernel, nt, fb, cw, gu_slots, dn_slots),
        out_shape=jax.ShapeDtypeStruct((rows, width), bf16),
        in_specs=[smem, smem, vmem, hbm, hbm, hbm],
        out_specs=vmem,
        scratch_shapes=[
            pltpu.VMEM((slots, rows, width + LANES), bf16),
            pltpu.VMEM((16, width + LANES), f32),
            pltpu.VMEM((total, width), bf16),
            pltpu.VMEM((total, LANES), f32),
            pltpu.VMEM((experts, total, hidden), bf16),
            pltpu.VMEM((gu_slots, 2, width, fb), bf16),
            pltpu.VMEM((dn_slots, experts, hidden, cw), bf16),
            pltpu.VMEM((nc, 2, total // 2, cw), f32),
            pltpu.VMEM((nc, total // 2, cw), bf16),
            pltpu.VMEM((nc, total // 2, cw), bf16),
            pltpu.VMEM((nc, nt, rows, cw), bf16),
            pltpu.VMEM((nc, nt, rows, cw), bf16),
            dma((gu_slots, 2)),
            dma((dn_slots, experts)),
            dma((nt,)),
            dma((nt,)),
            dma((slots,)),
            dma((nc,)),
            dma((nc,)),
            dma((nc, nt)),
            dma((nc, nt)),
        ],
        compiler_params=pltpu.CompilerParams(
            collective_id=0, has_side_effects=True, vmem_limit_bytes=VMEM_BYTES
        ),
    )(expert_ids.T, gate_ints.T, tokens, gate_weight, up_weight, down_weight)


def solution(mesh):
    return jax.shard_map(
        body,
        mesh=mesh,
        in_specs=(
            P(("rep", "exp", "tp"), None),
            P(("rep", "exp", "tp"), None),
            P(("rep", "exp", "tp"), None),
            P("exp", None, "tp"),
            P("exp", None, "tp"),
            P("exp", "tp", None),
        ),
        out_specs=P(("rep", "exp", "tp"), None),
        check_vma=False,
    )
```

```python
import functools

import jax
import jax.numpy as jnp
from jax import lax
from jax.experimental import pallas as pl
from jax.experimental.pallas import tpu as pltpu
from jax.sharding import PartitionSpec as P

MESH = pl.DeviceIdType.MESH
LANES = 128
VMEM_BYTES = 67043328


def kernel(
    nt, fb, cw, gu_slots, dn_slots,
    ids_ref, gates_ref, tok_ref, gw_ref, uw_ref, dw_ref, out_ref,
    xg, stage, x, wst, h, gu_buf, dn_buf,
    part, ex_send, ex_recv, tp_send, tp_recv,
    gu_sem, dn_sem, ga_send, ga_fwd, ga_recv, ex_ssem, ex_rsem, tp_ssem, tp_rsem,
):
    e = lax.axis_index("exp")
    t = lax.axis_index("tp")
    other = 1 - e
    me = e * nt + t
    pair = t + 1 - 2 * (t % 2)
    same = nt // 2
    rows, width = tok_ref.shape
    experts, _, hidden = gw_ref.shape
    tokens = x.shape[0]
    half = tokens // 2
    nf = hidden // fb
    nc = width // cw
    gu_steps = experts * nf

    def gu_copies(i, slot):
        l = i // nf
        columns = pl.ds(pl.multiple_of((i % nf) * fb, fb), fb) if nf > 1 else slice(None)
        return [
            pltpu.make_async_copy(
                ref.at[l, :, columns], gu_buf.at[slot, m], gu_sem.at[slot, m]
            )
            for m, ref in enumerate((gw_ref, uw_ref))
        ]

    def dn_copies(c, slot):
        c0 = pl.multiple_of(c * cw, cw)
        return [
            pltpu.make_async_copy(
                dw_ref.at[l, :, pl.ds(c0, cw)], dn_buf.at[slot, l], dn_sem.at[slot, l]
            )
            for l in range(experts)
        ]

    def first(i, carry):
        for copy in gu_copies(i, i):
            copy.start()
        return carry

    lax.fori_loop(0, gu_slots, first, 0)

    barrier = pltpu.get_barrier_semaphore()

    def greet(d, carry):
        pl.semaphore_signal(
            barrier, inc=1, device_id={"tp": (t + d) % nt}, device_id_type=MESH
        )
        return carry

    lax.fori_loop(1, nt, greet, 0)
    pl.semaphore_signal(barrier, inc=1, device_id={"exp": other}, device_id_type=MESH)

    lane = lax.broadcasted_iota(jnp.int32, (rows, LANES), 1)
    sub = lax.broadcasted_iota(jnp.int32, (rows, LANES), 0)
    weight = jnp.zeros((rows, LANES), jnp.float32)
    for r in range(rows):
        for k in range(ids_ref.shape[0]):
            value = gates_ref[k, r].astype(jnp.float32) * (1.0 / 256.0)
            weight += jnp.where((sub == r) & (lane == ids_ref[k, r]), value, 0.0)
    xg[me, :, :width] = tok_ref[...]
    xg[me, :, width:] = weight.astype(jnp.bfloat16)

    pl.semaphore_wait(barrier, nt)

    def to_other(tt):
        slot = e * nt + tt
        return pltpu.make_async_remote_copy(
            src_ref=xg.at[slot], dst_ref=xg.at[slot],
            send_sem=ga_fwd.at[tt], recv_sem=ga_recv.at[slot],
            device_id={"exp": other}, device_id_type=MESH,
        )

    def to_tp(d):
        return pltpu.make_async_remote_copy(
            src_ref=xg.at[me], dst_ref=xg.at[me],
            send_sem=ga_send.at[d], recv_sem=ga_recv.at[me],
            device_id={"tp": (t + 2 * d) % nt}, device_id_type=MESH,
        )

    def to_pair(d):
        slot = e * nt + (t + nt - 2 * d) % nt
        return pltpu.make_async_remote_copy(
            src_ref=xg.at[slot], dst_ref=xg.at[slot],
            send_sem=ga_send.at[same + d], recv_sem=ga_recv.at[slot],
            device_id={"tp": pair}, device_id_type=MESH,
        )

    def from_slot(slot):
        return pltpu.make_async_remote_copy(
            src_ref=xg.at[slot], dst_ref=xg.at[slot],
            send_sem=ga_send.at[0], recv_sem=ga_recv.at[slot],
            device_id={"exp": other}, device_id_type=MESH,
        )

    def push(d, carry):
        to_tp(d).start()
        return carry

    lax.fori_loop(1, same, push, 0)
    to_pair(0).start()
    to_other(t).start()

    def relay(d, carry):
        source = (t + nt - 2 * d) % nt
        from_slot(e * nt + source).wait_recv()
        to_pair(d).start()
        to_other(source).start()
        return carry

    lax.fori_loop(1, same, relay, 0)

    def hand_over(d, carry):
        source = (pair + nt - 2 * d) % nt
        from_slot(e * nt + source).wait_recv()
        to_other(source).start()
        return carry

    lax.fori_loop(0, same, hand_over, 0)

    def arrive(tt, carry):
        from_slot(other * nt + tt).wait_recv()
        return carry

    lax.fori_loop(0, nt, arrive, 0)

    group = stage.shape[0] // rows

    def lay(g, carry):
        for i in range(group):
            stage[i * rows:(i + 1) * rows, :] = xg[g * group + i].astype(jnp.float32)
        r0 = pl.multiple_of(g * group * rows, group * rows)
        x[pl.ds(r0, group * rows), :] = stage[:, :width].astype(jnp.bfloat16)
        wst[pl.ds(r0, group * rows), :] = stage[:, width:]
        return carry

    lax.fori_loop(0, tokens // (group * rows), lay, 0)

    def gu_step(i, carry):
        slot = i % gu_slots
        for copy in gu_copies(i, slot):
            copy.wait()
        gate, upper = (
            jnp.dot(x[...], gu_buf[slot, m], preferred_element_type=jnp.float32) for m in range(2)
        )
        columns = pl.ds(pl.multiple_of((i % nf) * fb, fb), fb) if nf > 1 else slice(None)
        h[i // nf, :, columns] = (gate / (1.0 + jnp.exp(-gate)) * upper).astype(jnp.bfloat16)
        later = i + gu_slots

        @pl.when(later < gu_steps)
        def _():
            for copy in gu_copies(later, slot):
                copy.start()

        column = later - gu_steps

        @pl.when((column >= 0) & (column < dn_slots))
        def _():
            for copy in dn_copies(column, column):
                copy.start()

        return carry

    lax.fori_loop(0, gu_steps, gu_step, 0)

    lanes = lax.broadcasted_iota(jnp.int32, (tokens, LANES), 1)
    scales = [
        jnp.sum(jnp.where(lanes == e * experts + l, wst[...], 0.0), axis=1, keepdims=True)
        for l in range(experts)
    ]

    def ex_copy(c):
        return pltpu.make_async_remote_copy(
            src_ref=ex_send.at[c], dst_ref=ex_recv.at[c],
            send_sem=ex_ssem.at[c], recv_sem=ex_rsem.at[c],
            device_id={"exp": other}, device_id_type=MESH,
        )

    def tp_copy(c, d):
        target = (t + d) % nt
        return pltpu.make_async_remote_copy(
            src_ref=tp_send.at[c, target], dst_ref=tp_recv.at[c, t],
            send_sem=tp_ssem.at[c, d], recv_sem=tp_rsem.at[c, t],
            device_id={"tp": target}, device_id_type=MESH,
        )

    def tp_from(c, source):
        return pltpu.make_async_remote_copy(
            src_ref=tp_send.at[c, source], dst_ref=tp_recv.at[c, source],
            send_sem=tp_ssem.at[c, 0], recv_sem=tp_rsem.at[c, source],
            device_id={"tp": source}, device_id_type=MESH,
        )

    def pass_on(c):
        ex_copy(c).wait_recv()
        total = part[c, e] + ex_recv[c].astype(jnp.float32)
        for j in range(nt):
            tp_send[c, j] = total[j * rows:(j + 1) * rows, :].astype(jnp.bfloat16)
        tp_recv[c, t] = tp_send[c, t]

        def send(d, carry):
            tp_copy(c, d).start()
            return carry

        lax.fori_loop(1, nt, send, 0)

    def dn_step(c, carry):
        slot = c % dn_slots
        for copy in dn_copies(c, slot):
            copy.wait()
        for n in range(0, cw, 256):
            size = min(256, cw - n)
            total = jnp.zeros((tokens, size), jnp.float32)
            for l in range(experts):
                total += scales[l] * jnp.dot(
                    h[l], dn_buf[slot, l, :, n:n + size], preferred_element_type=jnp.float32
                )
            part[c, 0, :, n:n + size] = total[:half]
            part[c, 1, :, n:n + size] = total[half:]
        ex_send[c] = part[c, other].astype(jnp.bfloat16)
        ex_copy(c).start()
        later = c + dn_slots

        @pl.when(later < nc)
        def _():
            for copy in dn_copies(later, slot):
                copy.start()

        @pl.when(c > 0)
        def _():
            pass_on(c - 1)

        return carry

    lax.fori_loop(0, nc, dn_step, 0)
    pass_on(nc - 1)

    for c in range(nc):
        def collect(d, carry, c=c):
            tp_from(c, (t + nt - d) % nt).wait_recv()
            return carry

        lax.fori_loop(1, nt, collect, 0)
        total = tp_recv[c, 0].astype(jnp.float32)
        for j in range(1, nt):
            total += tp_recv[c, j].astype(jnp.float32)
        out_ref[:, c * cw:(c + 1) * cw] = total.astype(out_ref.dtype)

    def finish(d, carry):
        to_other((t + d) % nt).wait_send()

        def drain(c, inner):
            tp_copy(c, d).wait_send()
            return inner

        lax.fori_loop(0, nc, drain, 0)
        return carry

    lax.fori_loop(1, nt, finish, 0)
    to_other(t).wait_send()
    to_pair(0).wait_send()

    def finish_gather(d, carry):
        to_tp(d).wait_send()
        to_pair(d).wait_send()
        return carry

    lax.fori_loop(1, same, finish_gather, 0)

    def drain_ex(c, carry):
        ex_copy(c).wait_send()
        return carry

    lax.fori_loop(0, nc, drain_ex, 0)


def body(tokens, expert_ids, gate_ints, gate_weight, up_weight, down_weight):
    rows, width = tokens.shape
    experts, _, hidden = gate_weight.shape
    nt = lax.axis_size("tp")
    slots = nt * lax.axis_size("exp")
    total = slots * rows
    fb = 256 if hidden % 256 == 0 else hidden
    cw = min(512, width)
    nf, nc = hidden // fb, width // cw
    gu_slots = min(8, experts * nf)
    dn_slots = min(7, nc)
    bf16, f32 = jnp.bfloat16, jnp.float32
    vmem = pl.BlockSpec(memory_space=pltpu.VMEM)
    smem = pl.BlockSpec(memory_space=pltpu.SMEM)
    hbm = pl.BlockSpec(memory_space=pl.ANY)
    dma = pltpu.SemaphoreType.DMA
    return pl.pallas_call(
        functools.partial(kernel, nt, fb, cw, gu_slots, dn_slots),
        out_shape=jax.ShapeDtypeStruct((rows, width), bf16),
        in_specs=[smem, smem, vmem, hbm, hbm, hbm],
        out_specs=vmem,
        scratch_shapes=[
            pltpu.VMEM((slots, rows, width + LANES), bf16),
            pltpu.VMEM((16, width + LANES), f32),
            pltpu.VMEM((total, width), bf16),
            pltpu.VMEM((total, LANES), f32),
            pltpu.VMEM((experts, total, hidden), bf16),
            pltpu.VMEM((gu_slots, 2, width, fb), bf16),
            pltpu.VMEM((dn_slots, experts, hidden, cw), bf16),
            pltpu.VMEM((nc, 2, total // 2, cw), f32),
            pltpu.VMEM((nc, total // 2, cw), bf16),
            pltpu.VMEM((nc, total // 2, cw), bf16),
            pltpu.VMEM((nc, nt, rows, cw), bf16),
            pltpu.VMEM((nc, nt, rows, cw), bf16),
            dma((gu_slots, 2)),
            dma((dn_slots, experts)),
            dma((nt,)),
            dma((nt,)),
            dma((slots,)),
            dma((nc,)),
            dma((nc,)),
            dma((nc, nt)),
            dma((nc, nt)),
        ],
        compiler_params=pltpu.CompilerParams(
            collective_id=0, has_side_effects=True, vmem_limit_bytes=VMEM_BYTES
        ),
    )(expert_ids.T, gate_ints.T, tokens, gate_weight, up_weight, down_weight)


def solution(mesh):
    return jax.shard_map(
        body,
        mesh=mesh,
        in_specs=(
            P(("rep", "exp", "tp"), None),
            P(("rep", "exp", "tp"), None),
            P(("rep", "exp", "tp"), None),
            P("exp", None, "tp"),
            P("exp", None, "tp"),
            P("exp", "tp", None),
        ),
        out_specs=P(("rep", "exp", "tp"), None),
        check_vma=False,
    )
```
